512 devices in a mesh: ctx: 32 (over y, x), tp: 16 (over z, core).
Axes of the slice: x: 4, y: 8, z: 8, core: 2. Of those that a mesh axis runs over, the one named last changes fastest.
Arguments:
- query_rows: bfloat16 [8192, 8192], P('ctx', 'tp'), may hold values from -15 to 15
- key_rows: bfloat16 [8192, 8192], P('ctx', 'tp'), may hold values from -6 to 6
- value_rows: bfloat16 [8192, 8192], P('ctx', 'tp'), may hold values from -54 to 54
- log_decay: float32 [64, 8192], P('tp', 'ctx'), may hold values from -1.6 to 0
- norm_gain: float32 [8192], P('tp'), may hold values from 0.1 to 1.9
- d_normed: bfloat16 [8192, 8192], P('ctx', 'tp'), may hold values from -6 to 6
Outputs:
- d_queries: bfloat16 [8192, 8192], P('ctx', 'tp')
- d_keys: bfloat16 [8192, 8192], P('ctx', 'tp')
- d_values: bfloat16 [8192, 8192], P('ctx', 'tp')
The draws below stay inside these ranges and needn't reach their ends.
All inputs are finite; a program needn't handle non-finite values.
Results may differ from the reference program's by a relative error of at most 0.01.
Values sent between devices are 32-bit elements; how exact they have to be, the bound alone decides.
No kernel may reach another device: no remote copies, remote signals or barrier semaphores. Data moves between devices by JAX's collectives and lax.ppermute only.
A program may use at most 64 MiB of HBM per device.

```python
import math
import jax
import jax.numpy as jnp
from jax import lax

HEADS = 64
DK = 128
BLOCK = 256
TOKENS = 8192


def draw_query_rows(key, part):
    key_rows, key_cells = jax.random.split(key)
    row_scale = jnp.exp(jax.random.uniform(key_rows, (TOKENS, 1), minval=math.log(0.5), maxval=math.log(5.0)))
    cells = jnp.clip(jax.random.normal(key_cells, (TOKENS, HEADS * DK)), -6.0, 6.0)
    return (0.5 * row_scale * cells).astype(jnp.float32).astype(jnp.bfloat16)


def draw_value_rows(key, part):
    key_cols, key_cells = jax.random.split(key)
    head_index = (jnp.arange(HEADS * DK) // DK).astype(jnp.float32)
    head_scale = jnp.power(3.0, head_index / (HEADS - 1))
    col_scale = jnp.exp(jax.random.uniform(key_cols, (HEADS * DK,), minval=math.log(0.3), maxval=math.log(3.0))) * head_scale
    cells = jnp.clip(jax.random.normal(key_cells, (TOKENS, HEADS * DK)), -6.0, 6.0)
    return (cells * col_scale[None, :]).astype(jnp.float32).astype(jnp.bfloat16)


def draw_log_decay(key, part):
    keys_all = jax.random.split(key, 7)
    fast_share = 0.5
    fast_heads = jax.random.uniform(keys_all[0], (HEADS,)) < fast_share
    fast_rate = jnp.exp(jax.random.uniform(keys_all[1], (HEADS,), minval=math.log(1.0 / 50.0), maxval=math.log(1.0 / 30.0)))
    slow_rate = jnp.exp(jax.random.uniform(keys_all[2], (HEADS,), minval=math.log(0.1), maxval=math.log(0.5))) / TOKENS
    baseline_decay_rate = jnp.where(fast_heads, fast_rate, slow_rate)
    block_decay_factor = jnp.exp(jax.random.uniform(keys_all[3], (HEADS, TOKENS // BLOCK), minval=math.log(0.5), maxval=math.log(2.0)))
    block_decay_factor = jnp.repeat(block_decay_factor, BLOCK, axis=1)
    token_decay_factor = jnp.exp(jax.random.uniform(keys_all[4], (HEADS, TOKENS), minval=math.log(0.5), maxval=math.log(2.0)))
    spike_locations = jax.random.randint(keys_all[5], (HEADS, 2), 0, TOKENS)
    spike_magnitude = jax.random.uniform(keys_all[6], (HEADS, 2), minval=0.2, maxval=0.5)
    token_offset = jnp.arange(TOKENS)
    sudden_spike = jnp.sum(jnp.where(token_offset[None, None, :] == spike_locations[:, :, None], -jnp.log(1.0 - spike_magnitude)[:, :, None], 0.0), axis=1)
    return (-(baseline_decay_rate[:, None] * block_decay_factor * token_decay_factor + sudden_spike)).astype(jnp.float32)


def levels(stream_key, shape, cuts, smallest, top_value):
    factor_of = 1.0
    for position, parts in cuts:
        draws = jax.random.uniform(jax.random.fold_in(jax.random.fold_in(stream_key, 6), position), (parts,), jnp.float32, smallest / len(cuts), top_value / len(cuts))
        factor_of = factor_of * jnp.repeat(jnp.exp(draws), shape[position] // parts).reshape((-1,) + (1,) * (len(shape) - 1 - position))
    return factor_of


def centred(stream_key, extent, width, most, pieces=(), kind=jnp.bfloat16):
    gain = levels(stream_key, extent, pieces, -0.22, 0.18) if pieces else 1.0
    array = jax.random.normal(stream_key, extent, jnp.float32) * width * gain
    return jnp.minimum(jnp.maximum(array, -most), most).astype(kind)


def setup_inputs(seed: int = 0) -> dict:
    keys = jax.random.split(jax.random.key(seed), 7)
    return {
        "query_rows": draw_query_rows(jax.random.fold_in(keys[6], 71), 0),
        "key_rows": centred(keys[1], (TOKENS, HEADS * DK), 0.5, 6.0, ((0, 32), (1, 16))),
        "value_rows": draw_value_rows(jax.random.fold_in(keys[6], 71), 0),
        "log_decay": draw_log_decay(jax.random.fold_in(keys[6], 71), 0),
        "norm_gain": jnp.clip(1.0 + 0.18 * jax.random.normal(keys[4], (HEADS * DK,), jnp.float32), 0.1, 1.9),
        "d_normed": centred(keys[5], (TOKENS, HEADS * DK), 0.5, 6.0, ((0, 32), (1, 16))),
    }


EPSILON = 1e-06

def rounded(value):
    return lax.optimization_barrier(value.astype(jnp.bfloat16)).astype(jnp.float32)

def block_tables(log_block):
    within = jnp.cumsum(log_block, axis=1)
    totals = within[:, -1]
    token_offset = jnp.arange(log_block.shape[1])
    causal = token_offset[:, None] >= token_offset[None, :]
    spread = within[:, :, None] - within[:, None, :]
    decay_mask = jnp.where(causal, jnp.exp(jnp.minimum(spread, 0.0)), 0.0)
    rise_scale = jnp.transpose(jnp.exp(within))[:, :, None]
    fall_scale = jnp.transpose(jnp.exp(totals[:, None] - within))[:, :, None]
    return (totals, decay_mask, rise_scale, fall_scale)

def forward_block(carried, block_in):
    query_block, key_block, value_block, log_block = block_in
    totals, decay_mask, rise_scale, fall_scale = block_tables(log_block)
    q_wide = query_block.astype(jnp.float32)
    k_wide = key_block.astype(jnp.float32)
    v_wide = value_block.astype(jnp.float32)
    q_decayed = rounded(query_block * rise_scale)
    k_decayed = rounded(key_block * fall_scale)
    scored = rounded(jnp.einsum('thd,shd->hts', q_wide, k_wide) * decay_mask)
    attended = jnp.einsum('hts,shd->thd', scored, v_wide) + jnp.einsum('thd,hde->the', q_decayed, rounded(carried))
    following = jnp.exp(totals)[:, None, None] * carried + jnp.einsum('shd,she->hde', k_decayed, v_wide)
    return (following, (attended.astype(jnp.bfloat16), carried))

def backward_block(grad_in, block_in):
    query_block, key_block, value_block, log_block, d_block, state_block = block_in
    totals, decay_mask, rise_scale, fall_scale = block_tables(log_block)
    q_wide = query_block.astype(jnp.float32)
    k_wide = key_block.astype(jnp.float32)
    v_wide = value_block.astype(jnp.float32)
    d_wide = d_block.astype(jnp.float32)
    q_decayed = rounded(query_block * rise_scale)
    k_decayed = rounded(key_block * fall_scale)
    scored = rounded(jnp.einsum('thd,shd->hts', q_wide, k_wide) * decay_mask)
    state_low = rounded(state_block)
    grad_low = rounded(grad_in)
    d_scored = rounded(jnp.einsum('the,she->hts', d_wide, v_wide) * decay_mask)
    d_query = jnp.einsum('hts,shd->thd', d_scored, k_wide) + rise_scale * jnp.einsum('the,hde->thd', d_wide, state_low)
    d_key = jnp.einsum('hts,thd->shd', d_scored, q_wide) + fall_scale * jnp.einsum('she,hde->shd', v_wide, grad_low)
    d_value = jnp.einsum('hts,the->she', scored, d_wide) + jnp.einsum('shd,hde->she', k_decayed, grad_low)
    earlier_grad = jnp.exp(totals)[:, None, None] * grad_in + jnp.einsum('thd,the->hde', q_decayed, d_wide)
    return (earlier_grad, (d_query.astype(jnp.bfloat16), d_key.astype(jnp.bfloat16), d_value.astype(jnp.bfloat16)))

def reference(query_rows, key_rows, value_rows, log_decay, norm_gain, d_normed):
    nblocks = TOKENS // BLOCK
    shape_four = (nblocks, BLOCK, HEADS, DK)
    queries = query_rows.reshape(shape_four)
    keyset = key_rows.reshape(shape_four)
    valueset = value_rows.reshape(shape_four)
    log_blocks = jnp.transpose(log_decay.reshape(HEADS, nblocks, BLOCK), (1, 0, 2))
    zero_state = jnp.zeros((HEADS, DK, DK), jnp.float32)
    final_state, (attended, states) = lax.scan(forward_block, zero_state, (queries, keyset, valueset, log_blocks))
    attended_wide = attended.astype(jnp.float32)
    gained = norm_gain.reshape(HEADS, DK) * d_normed.reshape(shape_four).astype(jnp.float32)
    squares = lax.optimization_barrier(jnp.sum(attended_wide * attended_wide, axis=(2, 3)))
    inner_sums = lax.optimization_barrier(jnp.sum(attended_wide * gained, axis=(2, 3)))
    features = HEADS * DK
    inv_rms = lax.rsqrt(squares / features + EPSILON)
    d_attended = (inv_rms[:, :, None, None] * gained - attended_wide * (inv_rms ** 3 * inner_sums / features)[:, :, None, None]).astype(jnp.bfloat16)
    first_grad, (d_query, d_key, d_value) = lax.scan(backward_block, zero_state, (queries, keyset, valueset, log_blocks, d_attended, states), reverse=True)
    flat_shape = (TOKENS, HEADS * DK)
    return (d_query.reshape(flat_shape), d_key.reshape(flat_shape), d_value.reshape(flat_shape))
```

```python
import functools

import jax
import jax.numpy as jnp
from jax import lax
from jax.experimental import pallas as pl
from jax.experimental.pallas import tpu as pltpu
from jax.sharding import PartitionSpec as P

DK = 128
BLOCK = 256
FEATURES = 8192
EPSILON = 1e-06
F32 = jnp.float32
BF16 = jnp.bfloat16


def dot(a, b, ca, cb):
    return lax.dot_general(a, b, (((ca,), (cb,)), ((), ())), preferred_element_type=F32)


def head(ref, h):
    return ref[:, h * DK : (h + 1) * DK]


def thirds(x):
    hi = x.astype(BF16)
    rest = x - hi.astype(F32)
    mid = rest.astype(BF16)
    lo = (rest - mid.astype(F32)).astype(BF16)
    return hi, mid, lo


def triangle():
    row = lax.broadcasted_iota(jnp.int32, (BLOCK, BLOCK), 0)
    col = lax.broadcasted_iota(jnp.int32, (BLOCK, BLOCK), 1)
    return row >= col


def cum_columns(log_decay, low):
    return sum(dot(low, part, 1, 1) for part in thirds(log_decay))


def cum_rows(log_decay, low):
    return sum(dot(part, low, 1, 1) for part in thirds(log_decay))


def update_kernel(k_ref, v_ref, ld_ref, kd_ref, update_ref, fade_ref):
    heads = ld_ref.shape[0]
    low = triangle().astype(F32).astype(BF16)
    cum = cum_columns(ld_ref[...], low)
    total = cum[BLOCK - 1 : BLOCK, :]
    fall = jnp.exp(total - cum)
    fade = jnp.exp(total)
    pieces = update_ref.shape[0] // heads
    for h in range(heads):
        kd = (head(k_ref, h).astype(F32) * fall[:, h : h + 1]).astype(BF16)
        kd_ref[:, h * DK : (h + 1) * DK] = kd
        update = dot(kd, head(v_ref, h), 0, 0)
        update_ref[h * pieces : (h + 1) * pieces] = update.reshape(pieces, -1, DK)
        fade_ref[h * pieces : (h + 1) * pieces] = jnp.broadcast_to(
            fade[:, h : h + 1].reshape(1, 1, 1), (pieces, 1, DK)
        )


def decay_mask(causal, columns, rows, h):
    spread = columns[:, h : h + 1] - rows[h : h + 1, :]
    return jnp.where(causal, jnp.exp(jnp.minimum(spread, 0.0)), 0.0)


def local_kernel(q_ref, k_ref, v_ref, ld_ref, qd_ref, scored_ref, local_ref):
    heads = ld_ref.shape[0]
    causal = triangle()
    low = causal.astype(F32).astype(BF16)
    columns = cum_columns(ld_ref[...], low)
    rows = cum_rows(ld_ref[...], low)
    rise = jnp.exp(columns)
    for h in range(heads):
        q = head(q_ref, h)
        qd_ref[:, h * DK : (h + 1) * DK] = (q.astype(F32) * rise[:, h : h + 1]).astype(BF16)
        scores = dot(q, head(k_ref, h), 1, 1)
        scored = (scores * decay_mask(causal, columns, rows, h)).astype(BF16)
        scored_ref[h] = scored
        local_ref[:, h * DK : (h + 1) * DK] = dot(scored, head(v_ref, h), 1, 0)


def scan_kernel(reverse, fade_ref, update_ref, before_ref):
    size = update_ref.shape[0]
    carried = jnp.zeros(update_ref.shape[1:], F32)
    for step in range(size):
        at = size - 1 - step if reverse else step
        before_ref[at] = carried
        carried = carried * fade_ref[at] + update_ref[at]


def attend_kernel(local_ref, qd_ref, state_ref, gain_ref, dn_ref, att_ref, sums_ref):
    heads = state_ref.shape[0]
    squares = jnp.zeros((BLOCK, DK), F32)
    inner = jnp.zeros((BLOCK, DK), F32)
    for h in range(heads):
        att = head(local_ref, h) + dot(head(qd_ref, h), state_ref[h].astype(BF16), 1, 0)
        att = att.astype(BF16)
        att_ref[:, h * DK : (h + 1) * DK] = att
        wide = att.astype(F32)
        gained = head(gain_ref, h) * head(dn_ref, h).astype(F32)
        squares += wide * wide
        inner += wide * gained
    squares = jnp.sum(jnp.transpose(squares), axis=0, keepdims=True)
    inner = jnp.sum(jnp.transpose(inner), axis=0, keepdims=True)
    mine = jnp.concatenate(
        [squares[:, :DK], squares[:, DK:], inner[:, :DK], inner[:, DK:]], axis=0
    )
    sums_ref[...] = jnp.broadcast_to(mine[None], sums_ref.shape)


def norm_kernel(att_ref, qd_ref, gain_ref, dn_ref, sums_ref, da_ref, update_ref):
    heads = att_ref.shape[1] // DK
    pieces = update_ref.shape[0] // heads
    sums = jnp.sum(sums_ref[...], axis=0)
    squares, inner = sums[0:2], sums[2:4]
    inv_rms = lax.rsqrt(squares * (1.0 / FEATURES) + EPSILON)
    pull = inv_rms * inv_rms * inv_rms * inner * (1.0 / FEATURES)
    scales = jnp.transpose(jnp.concatenate([inv_rms, pull, inv_rms, pull], axis=0))
    inv_rms = jnp.concatenate([scales[:, 0:1], scales[:, 1:2]], axis=0)
    pull = jnp.concatenate([scales[:, 2:3], scales[:, 3:4]], axis=0)
    for h in range(heads):
        gained = head(gain_ref, h) * head(dn_ref, h).astype(F32)
        da = (inv_rms * gained - head(att_ref, h).astype(F32) * pull).astype(BF16)
        da_ref[:, h * DK : (h + 1) * DK] = da
        update = dot(head(qd_ref, h), da, 0, 0)
        update_ref[h * pieces : (h + 1) * pieces] = update.reshape(pieces, -1, DK)


def grads_kernel(
    q_ref, k_ref, v_ref, ld_ref, scored_ref, state_ref, da_ref, dq_ref, dk_ref, dv_ref
):
    heads = ld_ref.shape[0]
    causal = triangle()
    low = causal.astype(F32).astype(BF16)
    columns = cum_columns(ld_ref[...], low)
    rows = cum_rows(ld_ref[...], low)
    rise = jnp.exp(columns)
    for h in range(heads):
        da = head(da_ref, h)
        here = slice(h * DK, (h + 1) * DK)
        d_scores = dot(da, head(v_ref, h), 1, 1)
        d_scored = (d_scores * decay_mask(causal, columns, rows, h)).astype(BF16)
        dq = dot(d_scored, head(k_ref, h), 1, 0)
        dq += rise[:, h : h + 1] * dot(da, state_ref[h].astype(BF16), 1, 1)
        dq_ref[:, here] = dq.astype(BF16)
        dk_ref[:, here] = dot(d_scored, head(q_ref, h), 0, 0)
        dv_ref[:, here] = dot(scored_ref[h], da, 0, 0)


def final_kernel(dk_local_ref, dv_local_ref, v_ref, kd_ref, ld_ref, grad_ref, dk_ref, dv_ref):
    heads = ld_ref.shape[0]
    low = triangle().astype(F32).astype(BF16)
    cum = cum_columns(ld_ref[...], low)
    fall = jnp.exp(cum[BLOCK - 1 : BLOCK, :] - cum)
    for h in range(heads):
        here = slice(h * DK, (h + 1) * DK)
        grad = grad_ref[h].astype(BF16)
        dk = head(dk_local_ref, h) + fall[:, h : h + 1] * dot(head(v_ref, h), grad, 1, 1)
        dk_ref[:, here] = dk.astype(BF16)
        dv = head(dv_local_ref, h) + dot(head(kd_ref, h), grad, 1, 0)
        dv_ref[:, here] = dv.astype(BF16)


def call(kernel, outs, flops, *args):
    moved = sum(a.size * a.dtype.itemsize for a in (*args, *outs))
    return pl.pallas_call(
        kernel,
        out_shape=outs,
        compiler_params=pltpu.CompilerParams(vmem_limit_bytes=32 << 20),
        cost_estimate=pl.CostEstimate(flops=flops, bytes_accessed=moved, transcendentals=0),
    )(*args)


def shape(dims, dtype=F32):
    return jax.ShapeDtypeStruct(dims, dtype)


def exchange(array, axis):
    return lax.all_to_all(array, axis, 0, 0, tiled=True)


def shards(query_rows, key_rows, value_rows, log_decay, norm_gain, d_normed):
    heads = log_decay.shape[0]
    ctx, tp = lax.axis_size("ctx"), lax.axis_size("tp")
    wide = heads * DK
    piece = heads * DK // ctx
    pieces = (ctx, piece, DK)
    rows, square = (BLOCK, wide), (heads, BLOCK, BLOCK)
    unit = 2 * heads * BLOCK * DK * DK
    gain = norm_gain.reshape(1, wide)

    k_decayed, updates, fade = call(
        update_kernel,
        (shape(rows, BF16), shape(pieces), shape((ctx, 1, DK))),
        unit,
        key_rows,
        value_rows,
        log_decay,
    )
    packed = jnp.concatenate([updates, fade], axis=1)[:, :, None, :]
    packed = exchange(packed, "ctx")
    fades = packed[:, piece:, 0, :]
    before = call(
        functools.partial(scan_kernel, False),
        (shape(pieces),),
        unit // 32,
        fades,
        packed[:, :piece, 0, :],
    )[0]
    q_decayed, scored, local = call(
        local_kernel,
        (shape(rows, BF16), shape(square, BF16), shape(rows)),
        6 * unit,
        query_rows,
        key_rows,
        value_rows,
        log_decay,
    )
    states = exchange(before, "ctx").reshape(heads, DK, DK)
    attended, sums = call(
        attend_kernel,
        (shape(rows, BF16), shape((tp, 4, DK))),
        unit,
        local,
        q_decayed,
        states,
        gain,
        d_normed,
    )
    sums = exchange(sums, "tp")
    d_attended, updates = call(
        norm_kernel,
        (shape(rows, BF16), shape(pieces)),
        unit,
        attended,
        q_decayed,
        gain,
        d_normed,
        sums,
    )
    after = call(
        functools.partial(scan_kernel, True),
        (shape(pieces),),
        unit // 32,
        fades,
        exchange(updates, "ctx"),
    )[0]
    d_query, dk_local, dv_local = call(
        grads_kernel,
        (shape(rows, BF16), shape(rows), shape(rows)),
        10 * unit,
        query_rows,
        key_rows,
        value_rows,
        log_decay,
        scored,
        states,
        d_attended,
    )
    grads = exchange(after, "ctx").reshape(heads, DK, DK)
    d_key, d_value = call(
        final_kernel,
        (shape(rows, BF16), shape(rows, BF16)),
        2 * unit,
        dk_local,
        dv_local,
        value_rows,
        k_decayed,
        log_decay,
        grads,
    )
    return d_query, d_key, d_value


def solution(mesh):
    placed = (
        P("ctx", "tp"),
        P("ctx", "tp"),
        P("ctx", "tp"),
        P("tp", "ctx"),
        P("tp"),
        P("ctx", "tp"),
    )
    return jax.shard_map(
        shards,
        mesh=mesh,
        in_specs=placed,
        out_specs=(P("ctx", "tp"), P("ctx", "tp"), P("ctx", "tp")),
        check_vma=False,
    )
```

```python
import functools

import jax
import jax.numpy as jnp
from jax import lax
from jax.experimental import pallas as pl
from jax.experimental.pallas import tpu as pltpu
from jax.sharding import PartitionSpec as P

DK = 128
BLOCK = 256
FEATURES = 8192
EPSILON = 1e-06
F32 = jnp.float32
BF16 = jnp.bfloat16


def dot(a, b, ca, cb):
    return lax.dot_general(a, b, (((ca,), (cb,)), ((), ())), preferred_element_type=F32)


def head(ref, h):
    return ref[:, h * DK : (h + 1) * DK]


def thirds(x):
    hi = x.astype(BF16)
    rest = x - hi.astype(F32)
    mid = rest.astype(BF16)
    lo = (rest - mid.astype(F32)).astype(BF16)
    return hi, mid, lo


def triangle():
    row = lax.broadcasted_iota(jnp.int32, (BLOCK, BLOCK), 0)
    col = lax.broadcasted_iota(jnp.int32, (BLOCK, BLOCK), 1)
    return row >= col


def cum_columns(log_decay, low):
    return sum(dot(low, part, 1, 1) for part in thirds(log_decay))


def cum_rows(log_decay, low):
    return sum(dot(part, low, 1, 1) for part in thirds(log_decay))


def update_kernel(k_hbm, v_hbm, ld_hbm, kd_ref, packed_ref, k_ref, v_ref, ld_ref, sems):
    heads = ld_ref.shape[0]
    copies = [pltpu.make_async_copy(ld_hbm, ld_ref, sems.at[2 * heads])]
    for h in range(heads):
        here = (slice(None), slice(h * DK, (h + 1) * DK))
        copies.append(pltpu.make_async_copy(k_hbm.at[here], k_ref.at[here], sems.at[2 * h]))
        copies.append(pltpu.make_async_copy(v_hbm.at[here], v_ref.at[here], sems.at[2 * h + 1]))
    for copy in copies:
        copy.start()
    low = triangle().astype(F32).astype(BF16)
    copies[0].wait()
    cum = cum_columns(ld_ref[...], low)
    total = cum[BLOCK - 1 : BLOCK, :]
    fall = jnp.exp(total - cum)
    fade = jnp.exp(total)
    pieces = packed_ref.shape[0] // heads
    piece = DK // pieces
    for h in range(heads):
        these = slice(h * pieces, (h + 1) * pieces)
        copies[2 * h + 1].wait()
        kd = (head(k_ref, h).astype(F32) * fall[:, h : h + 1]).astype(BF16)
        kd_ref[:, h * DK : (h + 1) * DK] = kd
        copies[2 * h + 2].wait()
        update = dot(kd, head(v_ref, h), 0, 0)
        packed_ref[these, 0:piece] = update.reshape(pieces, piece, 1, DK)
        packed_ref[these, piece : piece + 1] = jnp.broadcast_to(
            fade[:, h : h + 1].reshape(1, 1, 1, 1), (pieces, 1, 1, DK)
        )


def decay_mask(causal, columns, rows, h):
    spread = columns[:, h : h + 1] - rows[h : h + 1, :]
    return jnp.where(causal, jnp.exp(jnp.minimum(spread, 0.0)), 0.0)


def local_kernel(
    q_ref, k_ref, v_ref, ld_ref, gain_ref, dn_ref, qd_ref, scored_ref, local_ref, gained_ref
):
    gained_ref[...] = gain_ref[...] * dn_ref[...].astype(F32)
    heads = ld_ref.shape[0]
    causal = triangle()
    low = causal.astype(F32).astype(BF16)
    columns = cum_columns(ld_ref[...], low)
    rows = cum_rows(ld_ref[...], low)
    rise = jnp.exp(columns)
    for h in range(heads):
        q = head(q_ref, h)
        qd_ref[:, h * DK : (h + 1) * DK] = (q.astype(F32) * rise[:, h : h + 1]).astype(BF16)
        scores = dot(q, head(k_ref, h), 1, 1)
        scored = (scores * decay_mask(causal, columns, rows, h)).astype(BF16)
        scored_ref[h] = scored
        local_ref[:, h * DK : (h + 1) * DK] = dot(scored, head(v_ref, h), 1, 0)


def scan_kernel(reverse, fade_ref, update_ref, before_ref):
    size = update_ref.shape[0]
    carried = jnp.zeros(update_ref.shape[1:], F32)
    for step in range(size):
        at = size - 1 - step if reverse else step
        before_ref[at] = carried
        carried = carried * fade_ref[at] + update_ref[at]


def attend_kernel(local_ref, qd_ref, state_ref, gained_ref, att_ref, sums_ref):
    heads = state_ref.shape[0]
    squares = jnp.zeros((BLOCK, DK), F32)
    inner = jnp.zeros((BLOCK, DK), F32)
    for h in range(heads):
        att = head(local_ref, h) + dot(head(qd_ref, h), state_ref[h].astype(BF16), 1, 0)
        att = att.astype(BF16)
        att_ref[:, h * DK : (h + 1) * DK] = att
        wide = att.astype(F32)
        squares += wide * wide
        inner += wide * head(gained_ref, h)
    squares = jnp.sum(jnp.transpose(squares), axis=0, keepdims=True)
    inner = jnp.sum(jnp.transpose(inner), axis=0, keepdims=True)
    mine = jnp.concatenate(
        [squares[:, :DK], squares[:, DK:], inner[:, :DK], inner[:, DK:]], axis=0
    )
    sums_ref[...] = jnp.broadcast_to(mine[None], sums_ref.shape)


def norm_kernel(att_ref, qd_ref, gained_ref, sums_ref, da_ref, update_ref):
    heads = att_ref.shape[1] // DK
    pieces = update_ref.shape[0] // heads
    sums = jnp.sum(sums_ref[...], axis=0)
    squares, inner = sums[0:2], sums[2:4]
    inv_rms = lax.rsqrt(squares * (1.0 / FEATURES) + EPSILON)
    pull = inv_rms * inv_rms * inv_rms * inner * (1.0 / FEATURES)
    scales = jnp.transpose(jnp.concatenate([inv_rms, pull, inv_rms, pull], axis=0))
    inv_rms = jnp.concatenate([scales[:, 0:1], scales[:, 1:2]], axis=0)
    pull = jnp.concatenate([scales[:, 2:3], scales[:, 3:4]], axis=0)
    for h in range(heads):
        da = inv_rms * head(gained_ref, h) - head(att_ref, h).astype(F32) * pull
        da = da.astype(BF16)
        da_ref[:, h * DK : (h + 1) * DK] = da
        update = dot(head(qd_ref, h), da, 0, 0)
        update_ref[h * pieces : (h + 1) * pieces] = update.reshape(pieces, -1, DK)


def grads_kernel(
    q_ref, k_ref, v_ref, ld_ref, scored_ref, state_ref, da_ref, dq_ref, dk_ref, dv_ref
):
    heads = ld_ref.shape[0]
    causal = triangle()
    low = causal.astype(F32).astype(BF16)
    columns = cum_columns(ld_ref[...], low)
    rows = cum_rows(ld_ref[...], low)
    rise = jnp.exp(columns)
    for h in range(heads):
        da = head(da_ref, h)
        here = slice(h * DK, (h + 1) * DK)
        d_scores = dot(da, head(v_ref, h), 1, 1)
        d_scored = (d_scores * decay_mask(causal, columns, rows, h)).astype(BF16)
        dq = dot(d_scored, head(k_ref, h), 1, 0)
        dq += rise[:, h : h + 1] * dot(da, state_ref[h].astype(BF16), 1, 1)
        dq_ref[:, here] = dq.astype(BF16)
        dk_ref[:, here] = dot(d_scored, head(q_ref, h), 0, 0)
        dv_ref[:, here] = dot(scored_ref[h], da, 0, 0)


def final_kernel(
    dk_local_ref, dv_local_ref, v_ref, kd_ref, ld_ref, grad_ref, dk_hbm, dv_hbm, dk_ref, dv_ref, sems
):
    heads = ld_ref.shape[0]
    low = triangle().astype(F32).astype(BF16)
    cum = cum_columns(ld_ref[...], low)
    fall = jnp.exp(cum[BLOCK - 1 : BLOCK, :] - cum)
    copies = []
    for h in range(heads):
        here = (slice(None), slice(h * DK, (h + 1) * DK))
        grad = grad_ref[h].astype(BF16)
        dk = head(dk_local_ref, h) + fall[:, h : h + 1] * dot(head(v_ref, h), grad, 1, 1)
        dk_ref[here] = dk.astype(BF16)
        dv = head(dv_local_ref, h) + dot(head(kd_ref, h), grad, 1, 0)
        dv_ref[here] = dv.astype(BF16)
        copies.append(pltpu.make_async_copy(dk_ref.at[here], dk_hbm.at[here], sems.at[2 * h]))
        copies.append(pltpu.make_async_copy(dv_ref.at[here], dv_hbm.at[here], sems.at[2 * h + 1]))
        copies[-2].start()
        copies[-1].start()
    for copy in copies:
        copy.wait()


def call(kernel, outs, flops, *args, **kinds):
    moved = sum(a.size * a.dtype.itemsize for a in (*args, *outs))
    return pl.pallas_call(
        kernel,
        out_shape=outs,
        compiler_params=pltpu.CompilerParams(vmem_limit_bytes=8 << 20),
        cost_estimate=pl.CostEstimate(flops=flops, bytes_accessed=moved, transcendentals=0),
        **kinds,
    )(*args)


IN_HBM = pl.BlockSpec(memory_space=pltpu.HBM)


def shape(dims, dtype=F32):
    return jax.ShapeDtypeStruct(dims, dtype)


def exchange(array, axis):
    return lax.all_to_all(array, axis, 0, 0, tiled=True)


def shards(query_rows, key_rows, value_rows, log_decay, norm_gain, d_normed):
    heads = log_decay.shape[0]
    ctx, tp = lax.axis_size("ctx"), lax.axis_size("tp")
    wide = heads * DK
    piece = heads * DK // ctx
    pieces = (ctx, piece, DK)
    rows, square = (BLOCK, wide), (heads, BLOCK, BLOCK)
    unit = 2 * heads * BLOCK * DK * DK
    gain = norm_gain.reshape(1, wide)

    k_decayed, packed = call(
        update_kernel,
        (shape(rows, BF16), shape((ctx, piece + 1, 1, DK))),
        unit,
        *(pltpu.with_memory_space_constraint(x, pltpu.HBM) for x in (key_rows, value_rows, log_decay)),
        in_specs=[IN_HBM] * 3,
        scratch_shapes=[
            pltpu.VMEM(rows, BF16),
            pltpu.VMEM(rows, BF16),
            pltpu.VMEM(log_decay.shape, F32),
            pltpu.SemaphoreType.DMA((2 * heads + 1,)),
        ],
    )
    packed = exchange(packed, "ctx")
    fades = packed[:, piece:, 0, :]
    before = call(
        functools.partial(scan_kernel, False),
        (shape(pieces),),
        unit // 32,
        fades,
        packed[:, :piece, 0, :],
    )[0]
    q_decayed, scored, local, gained = call(
        local_kernel,
        (shape(rows, BF16), shape(square, BF16), shape(rows), shape(rows)),
        6 * unit,
        query_rows,
        key_rows,
        value_rows,
        log_decay,
        gain,
        d_normed,
    )
    states = exchange(before, "ctx").reshape(heads, DK, DK)
    attended, sums = call(
        attend_kernel,
        (shape(rows, BF16), shape((tp, 4, DK))),
        unit,
        local,
        q_decayed,
        states,
        gained,
    )
    sums = exchange(sums, "tp")
    d_attended, updates = call(
        norm_kernel,
        (shape(rows, BF16), shape(pieces)),
        unit,
        attended,
        q_decayed,
        gained,
        sums,
    )
    after = call(
        functools.partial(scan_kernel, True),
        (shape(pieces),),
        unit // 32,
        fades,
        exchange(updates, "ctx"),
    )[0]
    d_query, dk_local, dv_local = call(
        grads_kernel,
        (shape(rows, BF16), shape(rows), shape(rows)),
        10 * unit,
        query_rows,
        key_rows,
        value_rows,
        log_decay,
        scored,
        states,
        d_attended,
    )
    grads = exchange(after, "ctx").reshape(heads, DK, DK)
    d_key, d_value = call(
        final_kernel,
        (shape(rows, BF16), shape(rows, BF16)),
        2 * unit,
        dk_local,
        dv_local,
        value_rows,
        k_decayed,
        log_decay,
        grads,
        out_specs=(IN_HBM, IN_HBM),
        scratch_shapes=[
            pltpu.VMEM(rows, BF16),
            pltpu.VMEM(rows, BF16),
            pltpu.SemaphoreType.DMA((2 * heads,)),
        ],
    )
    return d_query, d_key, d_value


def solution(mesh):
    placed = (
        P("ctx", "tp"),
        P("ctx", "tp"),
        P("ctx", "tp"),
        P("tp", "ctx"),
        P("tp"),
        P("ctx", "tp"),
    )
    return jax.shard_map(
        shards,
        mesh=mesh,
        in_specs=placed,
        out_specs=(P("ctx", "tp"), P("ctx", "tp"), P("ctx", "tp")),
        check_vma=False,
    )
```

```python
import functools
import math

import jax
import jax.numpy as jnp
from jax import lax
from jax.experimental import pallas as pl
from jax.experimental.pallas import tpu as pltpu
from jax.sharding import PartitionSpec as P

DK = 128
BLOCK = 256
FEATURES = 8192
EPSILON = 1e-06
F32 = jnp.float32
BF16 = jnp.bfloat16


def dot(a, b, ca, cb):
    return lax.dot_general(a, b, (((ca,), (cb,)), ((), ())), preferred_element_type=F32)


def head(ref, h):
    return ref[:, h * DK : (h + 1) * DK]


def thirds(x):
    hi = x.astype(BF16)
    rest = x - hi.astype(F32)
    mid = rest.astype(BF16)
    lo = (rest - mid.astype(F32)).astype(BF16)
    return hi, mid, lo


def triangle():
    row = lax.broadcasted_iota(jnp.int32, (BLOCK, BLOCK), 0)
    col = lax.broadcasted_iota(jnp.int32, (BLOCK, BLOCK), 1)
    return row >= col


def cum_columns(log_decay, low):
    return sum(dot(low, part, 1, 1) for part in thirds(log_decay))


def cum_rows(log_decay, low):
    return sum(dot(part, low, 1, 1) for part in thirds(log_decay))


def update_kernel(k_hbm, v_hbm, ld_hbm, packed_ref, k_ref, v_ref, ld_ref, sems):
    heads = ld_ref.shape[0]
    pairs = ((ld_hbm, ld_ref), (k_hbm, k_ref), (v_hbm, v_ref))
    copies = [pltpu.make_async_copy(*pair, sems.at[i]) for i, pair in enumerate(pairs)]
    for copy in copies:
        copy.start()
    low = triangle().astype(F32).astype(BF16)
    copies[0].wait()
    cum = cum_rows(ld_ref[...], low)
    total = cum[:, BLOCK - 1 : BLOCK]
    fall = jnp.exp(total - cum)
    fade = jnp.exp(total)
    pieces = packed_ref.shape[0] // heads
    piece = DK // pieces
    copies[1].wait()
    kd = []
    for h in range(heads):
        flipped = jnp.transpose(head(k_ref, h)).astype(F32)
        kd.append((flipped * fall[h : h + 1, :]).astype(BF16))
    copies[2].wait()
    for h in range(heads):
        these = slice(h * pieces, (h + 1) * pieces)
        update = dot(kd[h], head(v_ref, h), 1, 0)
        packed_ref[these, 0:piece] = update.reshape(pieces, piece, 1, DK)
        packed_ref[these, piece : piece + 1] = jnp.broadcast_to(
            fade[h : h + 1, :].reshape(1, 1, 1, 1), (pieces, 1, 1, DK)
        )


def decay_mask(causal, columns, rows, h):
    spread = columns[:, h : h + 1] - rows[h : h + 1, :]
    return jnp.where(causal, jnp.exp(jnp.minimum(spread, 0.0)), 0.0)


def local_kernel(
    q_ref, k_ref, v_ref, ld_ref, gain_ref, dn_ref, qd_ref, flipped_ref, local_ref, gained_ref
):
    heads = ld_ref.shape[0]
    gained_ref[...] = gain_ref[...] * dn_ref[...].astype(F32)
    causal = triangle()
    low = causal.astype(F32).astype(BF16)
    columns = cum_columns(ld_ref[...], low)
    rows = cum_rows(ld_ref[...], low)
    rise = jnp.exp(columns)
    for h in range(heads):
        here = slice(h * DK, (h + 1) * DK)
        q = head(q_ref, h)
        qd = (q.astype(F32) * rise[:, h : h + 1]).astype(BF16)
        qd_ref[:, here] = qd
        flipped_ref[h] = jnp.transpose(qd)
        scored = dot(q, head(k_ref, h), 1, 1) * decay_mask(causal, columns, rows, h)
        local_ref[:, here] = dot(scored.astype(BF16), head(v_ref, h), 1, 0)


def scan_kernel(reverse, fade_ref, update_ref, before_ref):
    size = update_ref.shape[0]
    carried = jnp.zeros(update_ref.shape[1:], F32)
    for step in range(size):
        at = size - 1 - step if reverse else step
        before_ref[at] = carried
        carried = carried * fade_ref[at] + update_ref[at]


def attend_kernel(local_ref, qd_ref, state_ref, gained_ref, att_ref, sums_ref):
    heads = state_ref.shape[0]
    squares = jnp.zeros((BLOCK, DK), F32)
    inner = jnp.zeros((BLOCK, DK), F32)
    for h in range(heads):
        att = head(local_ref, h) + dot(head(qd_ref, h), state_ref[h].astype(BF16), 1, 0)
        att = att.astype(BF16)
        att_ref[:, h * DK : (h + 1) * DK] = att
        wide = att.astype(F32)
        squares += wide * wide
        inner += wide * head(gained_ref, h)
    squares = jnp.sum(jnp.transpose(squares), axis=0, keepdims=True)
    inner = jnp.sum(jnp.transpose(inner), axis=0, keepdims=True)
    mine = jnp.concatenate(
        [squares[:, :DK], squares[:, DK:], inner[:, :DK], inner[:, DK:]], axis=0
    )
    sums_ref[...] = jnp.broadcast_to(mine[None], sums_ref.shape)


def norm_kernel(att_ref, flipped_ref, gained_ref, sums_ref, da_ref, update_ref):
    heads = att_ref.shape[1] // DK
    pieces = update_ref.shape[0] // heads
    sums = jnp.sum(sums_ref[...], axis=0)
    squares, inner = sums[0:2], sums[2:4]
    inv_rms = lax.rsqrt(squares * (1.0 / FEATURES) + EPSILON)
    pull = inv_rms * inv_rms * inv_rms * inner * (1.0 / FEATURES)
    scales = jnp.transpose(jnp.concatenate([inv_rms, pull, inv_rms, pull], axis=0))
    inv_rms = jnp.concatenate([scales[:, 0:1], scales[:, 1:2]], axis=0)
    pull = jnp.concatenate([scales[:, 2:3], scales[:, 3:4]], axis=0)
    for h in range(heads):
        da = inv_rms * head(gained_ref, h) - head(att_ref, h).astype(F32) * pull
        da = da.astype(BF16)
        da_ref[:, h * DK : (h + 1) * DK] = da
        update = dot(flipped_ref[h], da, 1, 0)
        update_ref[h * pieces : (h + 1) * pieces] = update.reshape(pieces, -1, DK)


def grads_kernel(
    q_ref, k_ref, v_ref, ld_ref, state_ref, da_ref, dq_ref, kd_ref, fall_ref, dk_ref, dv_ref
):
    heads = ld_ref.shape[0]
    causal = triangle()
    low = causal.astype(F32).astype(BF16)
    columns = cum_columns(ld_ref[...], low)
    rows = cum_rows(ld_ref[...], low)
    rise = jnp.exp(columns)
    fall = jnp.exp(columns[BLOCK - 1 : BLOCK, :] - columns)
    for h in range(heads):
        here = slice(h * DK, (h + 1) * DK)
        q, k, da = head(q_ref, h), head(k_ref, h), head(da_ref, h)
        fall_wide = jnp.broadcast_to(fall[:, h : h + 1], (BLOCK, DK))
        fall_ref[:, here] = fall_wide
        kd_ref[:, here] = (k.astype(F32) * fall_wide).astype(BF16)
        mask = decay_mask(causal, columns, rows, h)
        scored = (dot(q, k, 1, 1) * mask).astype(BF16)
        d_scored = (dot(da, head(v_ref, h), 1, 1) * mask).astype(BF16)
        dq = dot(d_scored, k, 1, 0)
        dq += rise[:, h : h + 1] * dot(da, state_ref[h].astype(BF16), 1, 1)
        dq_ref[:, here] = dq.astype(BF16)
        dk_ref[:, here] = dot(d_scored, q, 0, 0)
        dv_ref[:, here] = dot(scored, da, 0, 0)


def final_kernel(
    dk_local_ref, dv_local_ref, v_ref, kd_ref, fall_ref, grad_ref, dk_hbm, dv_hbm, dk_ref, dv_ref, sems
):
    heads = grad_ref.shape[0]
    copies = []
    for h in range(heads):
        here = (slice(None), slice(h * DK, (h + 1) * DK))
        grad = grad_ref[h].astype(BF16)
        dk = head(dk_local_ref, h) + head(fall_ref, h) * dot(head(v_ref, h), grad, 1, 1)
        dk_ref[here] = dk.astype(BF16)
        dv = head(dv_local_ref, h) + dot(head(kd_ref, h), grad, 1, 0)
        dv_ref[here] = dv.astype(BF16)
        copies.append(pltpu.make_async_copy(dk_ref.at[here], dk_hbm.at[here], sems.at[2 * h]))
        copies.append(pltpu.make_async_copy(dv_ref.at[here], dv_hbm.at[here], sems.at[2 * h + 1]))
        copies[-2].start()
        copies[-1].start()
    for copy in copies:
        copy.wait()


def call(kernel, outs, flops, *args, **kinds):
    moved = sum(math.prod(a.shape) * 4 for a in (*args, *outs))
    return pl.pallas_call(
        kernel,
        out_shape=outs,
        compiler_params=pltpu.CompilerParams(vmem_limit_bytes=8 << 20),
        cost_estimate=pl.CostEstimate(flops=flops, bytes_accessed=moved, transcendentals=0),
        **kinds,
    )(*args)


IN_HBM = pl.BlockSpec(memory_space=pltpu.HBM)


def shape(dims, dtype=F32):
    return jax.ShapeDtypeStruct(dims, dtype)


def exchange(array, axis):
    return lax.all_to_all(array, axis, 0, 0, tiled=True)


def shards(query_rows, key_rows, value_rows, log_decay, norm_gain, d_normed):
    heads = log_decay.shape[0]
    ctx, tp = lax.axis_size("ctx"), lax.axis_size("tp")
    wide = heads * DK
    piece = heads * DK // ctx
    pieces = (ctx, piece, DK)
    rows = (BLOCK, wide)
    unit = 2 * heads * BLOCK * DK * DK
    gain = norm_gain.reshape(1, wide)

    packed = call(
        update_kernel,
        (shape((ctx, piece + 1, 1, DK)),),
        unit,
        *(pltpu.with_memory_space_constraint(x, pltpu.HBM) for x in (key_rows, value_rows, log_decay)),
        in_specs=[IN_HBM] * 3,
        scratch_shapes=[
            pltpu.VMEM(rows, BF16),
            pltpu.VMEM(rows, BF16),
            pltpu.VMEM(log_decay.shape, F32),
            pltpu.SemaphoreType.DMA((3,)),
        ],
    )[0]
    packed = exchange(packed, "ctx")
    fades = packed[:, piece:, 0, :]
    before = call(
        functools.partial(scan_kernel, False),
        (shape(pieces),),
        unit // 32,
        fades,
        packed[:, :piece, 0, :],
    )[0]
    q_decayed, flipped, local, gained = call(
        local_kernel,
        (shape(rows, BF16), shape((heads, DK, BLOCK), BF16), shape(rows), shape(rows)),
        6 * unit,
        query_rows,
        key_rows,
        value_rows,
        log_decay,
        gain,
        d_normed,
    )
    states = exchange(before, "ctx").reshape(heads, DK, DK)
    attended, sums = call(
        attend_kernel,
        (shape(rows, BF16), shape((tp, 4, DK))),
        unit,
        local,
        q_decayed,
        states,
        gained,
    )
    sums = exchange(sums, "tp")
    d_attended, updates = call(
        norm_kernel,
        (shape(rows, BF16), shape(pieces)),
        unit,
        attended,
        flipped,
        gained,
        sums,
    )
    after = call(
        functools.partial(scan_kernel, True),
        (shape(pieces),),
        unit // 32,
        fades,
        exchange(updates, "ctx"),
    )[0]
    d_query, k_decayed, fall, dk_local, dv_local = call(
        grads_kernel,
        (shape(rows, BF16), shape(rows, BF16), shape(rows), shape(rows), shape(rows)),
        12 * unit,
        query_rows,
        key_rows,
        value_rows,
        log_decay,
        states,
        d_attended,
    )
    grads = exchange(after, "ctx").reshape(heads, DK, DK)
    d_key, d_value = call(
        final_kernel,
        (shape(rows, BF16), shape(rows, BF16)),
        2 * unit,
        dk_local,
        dv_local,
        value_rows,
        k_decayed,
        fall,
        grads,
        out_specs=(IN_HBM, IN_HBM),
        scratch_shapes=[
            pltpu.VMEM(rows, BF16),
            pltpu.VMEM(rows, BF16),
            pltpu.SemaphoreType.DMA((2 * heads,)),
        ],
    )
    return d_query, d_key, d_value


def solution(mesh):
    placed = (
        P("ctx", "tp"),
        P("ctx", "tp"),
        P("ctx", "tp"),
        P("tp", "ctx"),
        P("tp"),
        P("ctx", "tp"),
    )
    return jax.shard_map(
        shards,
        mesh=mesh,
        in_specs=placed,
        out_specs=(P("ctx", "tp"), P("ctx", "tp"), P("ctx", "tp")),
        check_vma=False,
    )
```

```python
import functools
import math

import jax
import jax.numpy as jnp
from jax import lax
from jax.experimental import pallas as pl
from jax.experimental.pallas import tpu as pltpu
from jax.sharding import PartitionSpec as P

DK = 128
BLOCK = 256
FEATURES = 8192
EPSILON = 1e-06
F32 = jnp.float32
BF16 = jnp.bfloat16


def dot(a, b, ca, cb):
    return lax.dot_general(a, b, (((ca,), (cb,)), ((), ())), preferred_element_type=F32)


def head(ref, h):
    return ref[:, h * DK : (h + 1) * DK]


def thirds(x):
    hi = x.astype(BF16)
    rest = x - hi.astype(F32)
    mid = rest.astype(BF16)
    lo = (rest - mid.astype(F32)).astype(BF16)
    return hi, mid, lo


def triangle():
    row = lax.broadcasted_iota(jnp.int32, (BLOCK, BLOCK), 0)
    col = lax.broadcasted_iota(jnp.int32, (BLOCK, BLOCK), 1)
    return row >= col


def cum_columns(log_decay, low):
    return sum(dot(low, part, 1, 1) for part in thirds(log_decay))


def cum_rows(log_decay, low):
    return sum(dot(part, low, 1, 1) for part in thirds(log_decay))


def update_kernel(k_hbm, v_hbm, ld_hbm, packed_ref, k_ref, v_ref, ld_ref, sems):
    heads = ld_ref.shape[0]
    pairs = ((ld_hbm, ld_ref), (k_hbm, k_ref), (v_hbm, v_ref))
    copies = [pltpu.make_async_copy(*pair, sems.at[i]) for i, pair in enumerate(pairs)]
    for copy in copies:
        copy.start()
    low = triangle().astype(F32).astype(BF16)
    copies[0].wait()
    cum = cum_rows(ld_ref[...], low)
    total = cum[:, BLOCK - 1 : BLOCK]
    fall = jnp.exp(total - cum)
    fade = jnp.exp(total)
    pieces = packed_ref.shape[0] // heads
    piece = DK // pieces
    copies[1].wait()
    kd = []
    for h in range(heads):
        flipped = jnp.transpose(head(k_ref, h)).astype(F32)
        kd.append((flipped * fall[h : h + 1, :]).astype(BF16))
    copies[2].wait()
    for h in range(heads):
        these = slice(h * pieces, (h + 1) * pieces)
        update = dot(kd[h], head(v_ref, h), 1, 0)
        packed_ref[these, 0:piece] = update.reshape(pieces, piece, 1, DK)
        packed_ref[these, piece : piece + 1] = jnp.broadcast_to(
            fade[h : h + 1, :].reshape(1, 1, 1, 1), (pieces, 1, 1, DK)
        )


def decay_mask(causal, columns, rows, h):
    spread = columns[:, h : h + 1] - rows[h : h + 1, :]
    return jnp.where(causal, jnp.exp(jnp.minimum(spread, 0.0)), 0.0)


def local_kernel(
    q_ref, k_ref, v_ref, ld_ref, gain_ref, dn_ref, qd_ref, flipped_ref, local_ref, gained_ref
):
    heads = ld_ref.shape[0]
    gained_ref[...] = gain_ref[...] * dn_ref[...].astype(F32)
    causal = triangle()
    low = causal.astype(F32).astype(BF16)
    columns = cum_columns(ld_ref[...], low)
    rows = cum_rows(ld_ref[...], low)
    rise = jnp.exp(columns)
    for h in range(heads):
        here = slice(h * DK, (h + 1) * DK)
        q = head(q_ref, h)
        qd = (q.astype(F32) * rise[:, h : h + 1]).astype(BF16)
        qd_ref[:, here] = qd
        flipped_ref[h] = jnp.transpose(qd)
        scored = dot(q, head(k_ref, h), 1, 1) * decay_mask(causal, columns, rows, h)
        local_ref[:, here] = dot(scored.astype(BF16), head(v_ref, h), 1, 0)


def scan_kernel(order, fade_ref, update_ref, before_ref):
    carried = jnp.zeros(update_ref.shape[1:], F32)
    for at in order:
        before_ref[at] = carried
        carried = carried * fade_ref[at] + update_ref[at]


def attend_kernel(local_ref, qd_ref, state_ref, gained_ref, att_ref, sums_ref):
    heads = state_ref.shape[0]
    squares = jnp.zeros((BLOCK, DK), F32)
    inner = jnp.zeros((BLOCK, DK), F32)
    for h in range(heads):
        att = head(local_ref, h) + dot(head(qd_ref, h), state_ref[h].astype(BF16), 1, 0)
        att = att.astype(BF16)
        att_ref[:, h * DK : (h + 1) * DK] = att
        wide = att.astype(F32)
        squares += wide * wide
        inner += wide * head(gained_ref, h)
    squares = jnp.sum(jnp.transpose(squares), axis=0, keepdims=True)
    inner = jnp.sum(jnp.transpose(inner), axis=0, keepdims=True)
    mine = jnp.concatenate(
        [squares[:, :DK], squares[:, DK:], inner[:, :DK], inner[:, DK:]], axis=0
    )
    sums_ref[...] = jnp.broadcast_to(mine[None], sums_ref.shape)


def norm_kernel(att_ref, flipped_ref, gained_ref, sums_ref, da_ref, update_ref):
    heads = att_ref.shape[1] // DK
    pieces = update_ref.shape[0] // heads
    sums = jnp.sum(sums_ref[...], axis=0)
    squares, inner = sums[0:2], sums[2:4]
    inv_rms = lax.rsqrt(squares * (1.0 / FEATURES) + EPSILON)
    pull = inv_rms * inv_rms * inv_rms * inner * (1.0 / FEATURES)
    scales = jnp.transpose(jnp.concatenate([inv_rms, pull, inv_rms, pull], axis=0))
    inv_rms = jnp.concatenate([scales[:, 0:1], scales[:, 1:2]], axis=0)
    pull = jnp.concatenate([scales[:, 2:3], scales[:, 3:4]], axis=0)
    for h in range(heads):
        da = inv_rms * head(gained_ref, h) - head(att_ref, h).astype(F32) * pull
        da = da.astype(BF16)
        da_ref[:, h * DK : (h + 1) * DK] = da
        update = dot(flipped_ref[h], da, 1, 0)
        update_ref[h * pieces : (h + 1) * pieces] = update.reshape(pieces, -1, DK)


def grads_kernel(
    q_ref, k_ref, v_ref, ld_ref, state_ref, da_ref, dq_ref, kd_ref, fall_ref, dk_ref, dv_ref
):
    heads = ld_ref.shape[0]
    causal = triangle()
    low = causal.astype(F32).astype(BF16)
    columns = cum_columns(ld_ref[...], low)
    rows = cum_rows(ld_ref[...], low)
    rise = jnp.exp(columns)
    fall = jnp.exp(columns[BLOCK - 1 : BLOCK, :] - columns)
    for h in range(heads):
        here = slice(h * DK, (h + 1) * DK)
        q, k, da = head(q_ref, h), head(k_ref, h), head(da_ref, h)
        fall_wide = jnp.broadcast_to(fall[:, h : h + 1], (BLOCK, DK))
        fall_ref[:, here] = fall_wide
        kd_ref[:, here] = (k.astype(F32) * fall_wide).astype(BF16)
        mask = decay_mask(causal, columns, rows, h)
        scored = (dot(q, k, 1, 1) * mask).astype(BF16)
        d_scored = (dot(da, head(v_ref, h), 1, 1) * mask).astype(BF16)
        dq = dot(d_scored, k, 1, 0)
        dq += rise[:, h : h + 1] * dot(da, state_ref[h].astype(BF16), 1, 1)
        dq_ref[:, here] = dq.astype(BF16)
        dk_ref[:, here] = dot(d_scored, q, 0, 0)
        dv_ref[:, here] = dot(scored, da, 0, 0)


def final_kernel(
    dk_local_ref, dv_local_ref, v_ref, kd_ref, fall_ref, grad_ref, dk_hbm, dv_hbm, dk_ref, dv_ref, sems
):
    heads = grad_ref.shape[0]
    copies = []
    for h in range(heads):
        here = (slice(None), slice(h * DK, (h + 1) * DK))
        grad = grad_ref[h].astype(BF16)
        dk = head(dk_local_ref, h) + head(fall_ref, h) * dot(head(v_ref, h), grad, 1, 1)
        dk_ref[here] = dk.astype(BF16)
        dv = head(dv_local_ref, h) + dot(head(kd_ref, h), grad, 1, 0)
        dv_ref[here] = dv.astype(BF16)
        copies.append(pltpu.make_async_copy(dk_ref.at[here], dk_hbm.at[here], sems.at[2 * h]))
        copies.append(pltpu.make_async_copy(dv_ref.at[here], dv_hbm.at[here], sems.at[2 * h + 1]))
        copies[-2].start()
        copies[-1].start()
    for copy in copies:
        copy.wait()


def call(kernel, outs, flops, *args, **kinds):
    moved = sum(math.prod(a.shape) * 4 for a in (*args, *outs))
    return pl.pallas_call(
        kernel,
        out_shape=outs,
        compiler_params=pltpu.CompilerParams(vmem_limit_bytes=8 << 20),
        cost_estimate=pl.CostEstimate(flops=flops, bytes_accessed=moved, transcendentals=0),
        **kinds,
    )(*args)


IN_HBM = pl.BlockSpec(memory_space=pltpu.HBM)


def shape(dims, dtype=F32):
    return jax.ShapeDtypeStruct(dims, dtype)


def member_order(size, first):
    return [(first + place) % size for place in range(size)]


def exchange(array, axis, order):
    return lax.all_to_all(array, axis, 0, 0, axis_index_groups=[order], tiled=True)


def shards(query_rows, key_rows, value_rows, log_decay, norm_gain, d_normed):
    heads = log_decay.shape[0]
    ctx, tp = lax.axis_size("ctx"), lax.axis_size("tp")
    wide = heads * DK
    piece = heads * DK // ctx
    pieces = (ctx, piece, DK)
    rows = (BLOCK, wide)
    unit = 2 * heads * BLOCK * DK * DK
    gain = norm_gain.reshape(1, wide)
    order, tp_order = member_order(ctx, ctx // 2 + 2), member_order(tp, tp // 2)
    places = [order.index(block) for block in range(ctx)]

    packed = call(
        update_kernel,
        (shape((ctx, piece + 1, 1, DK)),),
        unit,
        *(pltpu.with_memory_space_constraint(x, pltpu.HBM) for x in (key_rows, value_rows, log_decay)),
        in_specs=[IN_HBM] * 3,
        scratch_shapes=[
            pltpu.VMEM(rows, BF16),
            pltpu.VMEM(rows, BF16),
            pltpu.VMEM(log_decay.shape, F32),
            pltpu.SemaphoreType.DMA((3,)),
        ],
    )[0]
    packed = exchange(packed, "ctx", order)
    fades = packed[:, piece:, 0, :]
    before = call(
        functools.partial(scan_kernel, places),
        (shape(pieces),),
        unit // 32,
        fades,
        packed[:, :piece, 0, :],
    )[0]
    q_decayed, flipped, local, gained = call(
        local_kernel,
        (shape(rows, BF16), shape((heads, DK, BLOCK), BF16), shape(rows), shape(rows)),
        6 * unit,
        query_rows,
        key_rows,
        value_rows,
        log_decay,
        gain,
        d_normed,
    )
    states = exchange(before, "ctx", order).reshape(heads, DK, DK)
    attended, sums = call(
        attend_kernel,
        (shape(rows, BF16), shape((tp, 4, DK))),
        unit,
        local,
        q_decayed,
        states,
        gained,
    )
    sums = exchange(sums, "tp", tp_order)
    d_attended, updates = call(
        norm_kernel,
        (shape(rows, BF16), shape(pieces)),
        unit,
        attended,
        flipped,
        gained,
        sums,
    )
    after = call(
        functools.partial(scan_kernel, places[::-1]),
        (shape(pieces),),
        unit // 32,
        fades,
        exchange(updates, "ctx", order),
    )[0]
    d_query, k_decayed, fall, dk_local, dv_local = call(
        grads_kernel,
        (shape(rows, BF16), shape(rows, BF16), shape(rows), shape(rows), shape(rows)),
        12 * unit,
        query_rows,
        key_rows,
        value_rows,
        log_decay,
        states,
        d_attended,
    )
    grads = exchange(after, "ctx", order).reshape(heads, DK, DK)
    d_key, d_value = call(
        final_kernel,
        (shape(rows, BF16), shape(rows, BF16)),
        2 * unit,
        dk_local,
        dv_local,
        value_rows,
        k_decayed,
        fall,
        grads,
        out_specs=(IN_HBM, IN_HBM),
        scratch_shapes=[
            pltpu.VMEM(rows, BF16),
            pltpu.VMEM(rows, BF16),
            pltpu.SemaphoreType.DMA((2 * heads,)),
        ],
    )
    return d_query, d_key, d_value


def solution(mesh):
    placed = (
        P("ctx", "tp"),
        P("ctx", "tp"),
        P("ctx", "tp"),
        P("tp", "ctx"),
        P("tp"),
        P("ctx", "tp"),
    )
    return jax.shard_map(
        shards,
        mesh=mesh,
        in_specs=placed,
        out_specs=(P("ctx", "tp"), P("ctx", "tp"), P("ctx", "tp")),
        check_vma=False,
    )
```

```python
import functools
import math

import jax
import jax.numpy as jnp
from jax import lax
from jax.experimental import pallas as pl
from jax.experimental.pallas import tpu as pltpu
from jax.sharding import PartitionSpec as P

DK = 128
BLOCK = 256
FEATURES = 8192
EPSILON = 1e-06
F32 = jnp.float32
BF16 = jnp.bfloat16


def dot(a, b, ca, cb):
    return lax.dot_general(a, b, (((ca,), (cb,)), ((), ())), preferred_element_type=F32)


def head(ref, h):
    return ref[:, h * DK : (h + 1) * DK]


def thirds(x):
    hi = x.astype(BF16)
    rest = x - hi.astype(F32)
    mid = rest.astype(BF16)
    lo = (rest - mid.astype(F32)).astype(BF16)
    return hi, mid, lo


def triangle():
    row = lax.broadcasted_iota(jnp.int32, (BLOCK, BLOCK), 0)
    col = lax.broadcasted_iota(jnp.int32, (BLOCK, BLOCK), 1)
    return row >= col


def cum_columns(log_decay, low):
    return sum(dot(low, part, 1, 1) for part in thirds(log_decay))


def cum_rows(log_decay, low):
    return sum(dot(part, low, 1, 1) for part in thirds(log_decay))


def update_kernel(k_hbm, v_hbm, ld_hbm, packed_ref, k_ref, v_ref, ld_ref, sems):
    heads = ld_ref.shape[0]
    pairs = ((ld_hbm, ld_ref), (k_hbm, k_ref), (v_hbm, v_ref))
    copies = [pltpu.make_async_copy(*pair, sems.at[i]) for i, pair in enumerate(pairs)]
    for copy in copies:
        copy.start()
    low = triangle().astype(F32).astype(BF16)
    copies[0].wait()
    cum = cum_rows(ld_ref[...], low)
    total = cum[:, BLOCK - 1 : BLOCK]
    fall = jnp.exp(total - cum)
    fade = jnp.exp(total)
    pieces = packed_ref.shape[0] // heads
    piece = DK // pieces
    copies[1].wait()
    kd = []
    for h in range(heads):
        flipped = jnp.transpose(head(k_ref, h)).astype(F32)
        kd.append((flipped * fall[h : h + 1, :]).astype(BF16))
    copies[2].wait()
    for h in range(heads):
        these = slice(h * pieces, (h + 1) * pieces)
        update = dot(kd[h], head(v_ref, h), 1, 0)
        packed_ref[these, 0:piece] = update.reshape(pieces, piece, 1, DK)
        packed_ref[these, piece : piece + 1] = jnp.broadcast_to(
            fade[h : h + 1, :].reshape(1, 1, 1, 1), (pieces, 1, 1, DK)
        )


def decay_mask(causal, columns, rows, h):
    spread = columns[:, h : h + 1] - rows[h : h + 1, :]
    return jnp.where(causal, jnp.exp(jnp.minimum(spread, 0.0)), 0.0)


def local_kernel(
    q_ref, k_ref, v_ref, ld_ref, gain_ref, dn_ref, qd_ref, flipped_ref, local_ref, gained_ref
):
    heads = ld_ref.shape[0]
    gained_ref[...] = gain_ref[...] * dn_ref[...].astype(F32)
    causal = triangle()
    low = causal.astype(F32).astype(BF16)
    columns = cum_columns(ld_ref[...], low)
    rows = cum_rows(ld_ref[...], low)
    rise = jnp.exp(columns)
    for h in range(heads):
        here = slice(h * DK, (h + 1) * DK)
        q = head(q_ref, h)
        qd = (q.astype(F32) * rise[:, h : h + 1]).astype(BF16)
        qd_ref[:, here] = qd
        flipped_ref[h] = jnp.transpose(qd)
        scored = dot(q, head(k_ref, h), 1, 1) * decay_mask(causal, columns, rows, h)
        local_ref[:, here] = dot(scored.astype(BF16), head(v_ref, h), 1, 0)


def scan_kernel(order, fade_ref, update_ref, before_ref):
    carried = jnp.zeros(update_ref.shape[1:], F32)
    for at in order:
        before_ref[at] = carried
        carried = carried * fade_ref[at] + update_ref[at]


def attend_kernel(local_ref, qd_ref, state_ref, gained_ref, att_ref, sums_ref):
    heads = state_ref.shape[0]
    squares = jnp.zeros((BLOCK, DK), F32)
    inner = jnp.zeros((BLOCK, DK), F32)
    for h in range(heads):
        att = head(local_ref, h) + dot(head(qd_ref, h), state_ref[h].astype(BF16), 1, 0)
        att = att.astype(BF16)
        att_ref[:, h * DK : (h + 1) * DK] = att
        wide = att.astype(F32)
        squares += wide * wide
        inner += wide * head(gained_ref, h)
    squares = jnp.sum(jnp.transpose(squares), axis=0, keepdims=True)
    inner = jnp.sum(jnp.transpose(inner), axis=0, keepdims=True)
    mine = jnp.concatenate(
        [squares[:, :DK], squares[:, DK:], inner[:, :DK], inner[:, DK:]], axis=0
    )
    sums_ref[...] = jnp.broadcast_to(mine[None], sums_ref.shape)


def norm_kernel(att_ref, flipped_ref, gained_ref, sums_ref, da_ref, update_ref):
    heads = att_ref.shape[1] // DK
    pieces = update_ref.shape[0] // heads
    sums = jnp.sum(sums_ref[...], axis=0)
    squares, inner = sums[0:2], sums[2:4]
    inv_rms = lax.rsqrt(squares * (1.0 / FEATURES) + EPSILON)
    pull = inv_rms * inv_rms * inv_rms * inner * (1.0 / FEATURES)
    scales = jnp.transpose(jnp.concatenate([inv_rms, pull, inv_rms, pull], axis=0))
    inv_rms = jnp.concatenate([scales[:, 0:1], scales[:, 1:2]], axis=0)
    pull = jnp.concatenate([scales[:, 2:3], scales[:, 3:4]], axis=0)
    for h in range(heads):
        da = inv_rms * head(gained_ref, h) - head(att_ref, h).astype(F32) * pull
        da = da.astype(BF16)
        da_ref[:, h * DK : (h + 1) * DK] = da
        update = dot(flipped_ref[h], da, 1, 0)
        update_ref[h * pieces : (h + 1) * pieces] = update.reshape(pieces, -1, DK)


def grads_kernel(
    q_ref, k_ref, v_ref, ld_ref, state_ref, da_ref, dq_ref, kd_ref, fall_ref, dk_ref, dv_ref
):
    heads = ld_ref.shape[0]
    causal = triangle()
    low = causal.astype(F32).astype(BF16)
    columns = cum_columns(ld_ref[...], low)
    rows = cum_rows(ld_ref[...], low)
    rise = jnp.exp(columns)
    fall = jnp.exp(columns[BLOCK - 1 : BLOCK, :] - columns)
    for h in range(heads):
        here = slice(h * DK, (h + 1) * DK)
        q, k, da = head(q_ref, h), head(k_ref, h), head(da_ref, h)
        fall_wide = jnp.broadcast_to(fall[:, h : h + 1], (BLOCK, DK))
        fall_ref[:, here] = fall_wide
        kd_ref[:, here] = (k.astype(F32) * fall_wide).astype(BF16)
        mask = decay_mask(causal, columns, rows, h)
        scored = (dot(q, k, 1, 1) * mask).astype(BF16)
        d_scored = (dot(da, head(v_ref, h), 1, 1) * mask).astype(BF16)
        dq = dot(d_scored, k, 1, 0)
        dq += rise[:, h : h + 1] * dot(da, state_ref[h].astype(BF16), 1, 1)
        dq_ref[:, here] = dq.astype(BF16)
        dk_ref[:, here] = dot(d_scored, q, 0, 0)
        dv_ref[:, here] = dot(scored, da, 0, 0)


def final_kernel(
    dk_local_ref, dv_local_ref, v_ref, kd_ref, fall_ref, grad_ref, dk_hbm, dv_hbm, dk_ref, dv_ref, sems
):
    heads = grad_ref.shape[0]
    copies = []
    for h in range(heads):
        here = (slice(None), slice(h * DK, (h + 1) * DK))
        grad = grad_ref[h].astype(BF16)
        dk = head(dk_local_ref, h) + head(fall_ref, h) * dot(head(v_ref, h), grad, 1, 1)
        dk_ref[here] = dk.astype(BF16)
        dv = head(dv_local_ref, h) + dot(head(kd_ref, h), grad, 1, 0)
        dv_ref[here] = dv.astype(BF16)
        copies.append(pltpu.make_async_copy(dk_ref.at[here], dk_hbm.at[here], sems.at[2 * h]))
        copies.append(pltpu.make_async_copy(dv_ref.at[here], dv_hbm.at[here], sems.at[2 * h + 1]))
        copies[-2].start()
        copies[-1].start()
    for copy in copies:
        copy.wait()


def call(kernel, outs, flops, *args, **kinds):
    moved = sum(math.prod(a.shape) * 4 for a in (*args, *outs))
    return pl.pallas_call(
        kernel,
        out_shape=outs,
        compiler_params=pltpu.CompilerParams(vmem_limit_bytes=8 << 20),
        cost_estimate=pl.CostEstimate(flops=flops, bytes_accessed=moved, transcendentals=0),
        **kinds,
    )(*args)


IN_HBM = pl.BlockSpec(memory_space=pltpu.HBM)


def shape(dims, dtype=F32):
    return jax.ShapeDtypeStruct(dims, dtype)


def member_order(size, first):
    return [(first + place) % size for place in range(size)]


def exchange(array, axis, order):
    return lax.all_to_all(array, axis, 0, 0, axis_index_groups=[order], tiled=True)


def shards(query_rows, key_rows, value_rows, log_decay, norm_gain, d_normed):
    heads = log_decay.shape[0]
    ctx, tp = lax.axis_size("ctx"), lax.axis_size("tp")
    wide = heads * DK
    piece = heads * DK // ctx
    pieces = (ctx, piece, DK)
    rows = (BLOCK, wide)
    unit = 2 * heads * BLOCK * DK * DK
    gain = norm_gain.reshape(1, wide)
    order = member_order(ctx, ctx // 2 + 2)
    chips = member_order(tp // 2, tp // 2 - 1)
    tp_order = [chip * 2 + core for core in (1, 0) for chip in chips]
    places = [order.index(block) for block in range(ctx)]

    packed = call(
        update_kernel,
        (shape((ctx, piece + 1, 1, DK)),),
        unit,
        *(pltpu.with_memory_space_constraint(x, pltpu.HBM) for x in (key_rows, value_rows, log_decay)),
        in_specs=[IN_HBM] * 3,
        scratch_shapes=[
            pltpu.VMEM(rows, BF16),
            pltpu.VMEM(rows, BF16),
            pltpu.VMEM(log_decay.shape, F32),
            pltpu.SemaphoreType.DMA((3,)),
        ],
    )[0]
    packed = exchange(packed, "ctx", order)
    fades = packed[:, piece:, 0, :]
    before = call(
        functools.partial(scan_kernel, places),
        (shape(pieces),),
        unit // 32,
        fades,
        packed[:, :piece, 0, :],
    )[0]
    q_decayed, flipped, local, gained = call(
        local_kernel,
        (shape(rows, BF16), shape((heads, DK, BLOCK), BF16), shape(rows), shape(rows)),
        6 * unit,
        query_rows,
        key_rows,
        value_rows,
        log_decay,
        gain,
        d_normed,
    )
    states = exchange(before, "ctx", order).reshape(heads, DK, DK)
    attended, sums = call(
        attend_kernel,
        (shape(rows, BF16), shape((tp, 4, DK))),
        unit,
        local,
        q_decayed,
        states,
        gained,
    )
    sums = exchange(sums, "tp", tp_order)
    d_attended, updates = call(
        norm_kernel,
        (shape(rows, BF16), shape(pieces)),
        unit,
        attended,
        flipped,
        gained,
        sums,
    )
    after = call(
        functools.partial(scan_kernel, places[::-1]),
        (shape(pieces),),
        unit // 32,
        fades,
        exchange(updates, "ctx", order),
    )[0]
    d_query, k_decayed, fall, dk_local, dv_local = call(
        grads_kernel,
        (shape(rows, BF16), shape(rows, BF16), shape(rows), shape(rows), shape(rows)),
        12 * unit,
        query_rows,
        key_rows,
        value_rows,
        log_decay,
        states,
        d_attended,
    )
    grads = exchange(after, "ctx", order).reshape(heads, DK, DK)
    d_key, d_value = call(
        final_kernel,
        (shape(rows, BF16), shape(rows, BF16)),
        2 * unit,
        dk_local,
        dv_local,
        value_rows,
        k_decayed,
        fall,
        grads,
        out_specs=(IN_HBM, IN_HBM),
        scratch_shapes=[
            pltpu.VMEM(rows, BF16),
            pltpu.VMEM(rows, BF16),
            pltpu.SemaphoreType.DMA((2 * heads,)),
        ],
    )
    return d_query, d_key, d_value


def solution(mesh):
    placed = (
        P("ctx", "tp"),
        P("ctx", "tp"),
        P("ctx", "tp"),
        P("tp", "ctx"),
        P("tp"),
        P("ctx", "tp"),
    )
    return jax.shard_map(
        shards,
        mesh=mesh,
        in_specs=placed,
        out_specs=(P("ctx", "tp"), P("ctx", "tp"), P("ctx", "tp")),
        check_vma=False,
    )
```

```python
import functools
import math

import jax
import jax.numpy as jnp
from jax import lax
from jax.experimental import pallas as pl
from jax.experimental.pallas import tpu as pltpu
from jax.sharding import PartitionSpec as P

DK = 128
BLOCK = 256
FEATURES = 8192
EPSILON = 1e-06
F32 = jnp.float32
BF16 = jnp.bfloat16


def dot(a, b, ca, cb):
    return lax.dot_general(a, b, (((ca,), (cb,)), ((), ())), preferred_element_type=F32)


def head(ref, h):
    return ref[:, h * DK : (h + 1) * DK]


def thirds(x):
    hi = x.astype(BF16)
    rest = x - hi.astype(F32)
    mid = rest.astype(BF16)
    lo = (rest - mid.astype(F32)).astype(BF16)
    return hi, mid, lo


def triangle():
    row = lax.broadcasted_iota(jnp.int32, (BLOCK, BLOCK), 0)
    col = lax.broadcasted_iota(jnp.int32, (BLOCK, BLOCK), 1)
    return row >= col


def cum_columns(log_decay, low):
    return sum(dot(low, part, 1, 1) for part in thirds(log_decay))


def cum_rows(log_decay, low):
    return sum(dot(part, low, 1, 1) for part in thirds(log_decay))


def update_kernel(k_hbm, v_hbm, ld_hbm, packed_ref, k_ref, v_ref, ld_ref, sems):
    heads = ld_ref.shape[0]
    pairs = ((ld_hbm, ld_ref), (k_hbm, k_ref), (v_hbm, v_ref))
    copies = [pltpu.make_async_copy(*pair, sems.at[i]) for i, pair in enumerate(pairs)]
    for copy in copies:
        copy.start()
    low = triangle().astype(F32).astype(BF16)
    copies[0].wait()
    cum = cum_rows(ld_ref[...], low)
    total = cum[:, BLOCK - 1 : BLOCK]
    fall = jnp.exp(total - cum)
    fade = jnp.exp(total)
    pieces = packed_ref.shape[0] // heads
    piece = DK // pieces
    copies[1].wait()
    kd = []
    for h in range(heads):
        flipped = jnp.transpose(head(k_ref, h)).astype(F32)
        kd.append((flipped * fall[h : h + 1, :]).astype(BF16))
    copies[2].wait()
    for h in range(heads):
        these = slice(h * pieces, (h + 1) * pieces)
        update = dot(kd[h], head(v_ref, h), 1, 0)
        packed_ref[these, 0:piece] = update.reshape(pieces, piece, 1, DK)
        packed_ref[these, piece : piece + 1] = jnp.broadcast_to(
            fade[h : h + 1, :].reshape(1, 1, 1, 1), (pieces, 1, 1, DK)
        )


def decay_mask(causal, columns, rows, h):
    spread = columns[:, h : h + 1] - rows[h : h + 1, :]
    return jnp.where(causal, jnp.exp(jnp.minimum(spread, 0.0)), 0.0)


def local_kernel(
    q_ref, k_ref, v_ref, ld_ref, gain_ref, dn_ref, qd_ref, flipped_ref, local_ref, gained_ref
):
    heads = ld_ref.shape[0]
    gained_ref[...] = gain_ref[...] * dn_ref[...].astype(F32)
    causal = triangle()
    low = causal.astype(F32).astype(BF16)
    columns = cum_columns(ld_ref[...], low)
    rows = cum_rows(ld_ref[...], low)
    rise = jnp.exp(columns)
    for h in range(heads):
        here = slice(h * DK, (h + 1) * DK)
        q = head(q_ref, h)
        qd = (q.astype(F32) * rise[:, h : h + 1]).astype(BF16)
        qd_ref[:, here] = qd
        flipped_ref[h] = jnp.transpose(qd)
        scored = dot(q, head(k_ref, h), 1, 1) * decay_mask(causal, columns, rows, h)
        local_ref[:, here] = dot(scored.astype(BF16), head(v_ref, h), 1, 0)


def scan_kernel(order, fade_ref, update_ref, before_ref):
    carried = jnp.zeros(update_ref.shape[1:], F32)
    for at in order:
        before_ref[at] = carried
        carried = carried * fade_ref[at] + update_ref[at]


def attend_kernel(local_ref, qd_ref, state_ref, gained_ref, att_ref, sums_ref):
    heads = state_ref.shape[0]
    squares = jnp.zeros((BLOCK, DK), F32)
    inner = jnp.zeros((BLOCK, DK), F32)
    for h in range(heads):
        att = head(local_ref, h) + dot(head(qd_ref, h), state_ref[h].astype(BF16), 1, 0)
        att = att.astype(BF16)
        att_ref[:, h * DK : (h + 1) * DK] = att
        wide = att.astype(F32)
        squares += wide * wide
        inner += wide * head(gained_ref, h)
    squares = jnp.sum(jnp.transpose(squares), axis=0, keepdims=True)
    inner = jnp.sum(jnp.transpose(inner), axis=0, keepdims=True)
    mine = jnp.concatenate(
        [squares[:, :DK], squares[:, DK:], inner[:, :DK], inner[:, DK:]], axis=0
    )
    sums_ref[...] = jnp.broadcast_to(mine[None], sums_ref.shape)


def norm_kernel(att_ref, flipped_ref, gained_ref, sums_ref, da_ref, update_ref):
    heads = att_ref.shape[1] // DK
    pieces = update_ref.shape[0] // heads
    sums = jnp.sum(sums_ref[...], axis=0)
    squares, inner = sums[0:2], sums[2:4]
    inv_rms = lax.rsqrt(squares * (1.0 / FEATURES) + EPSILON)
    pull = inv_rms * inv_rms * inv_rms * inner * (1.0 / FEATURES)
    scales = jnp.transpose(jnp.concatenate([inv_rms, pull, inv_rms, pull], axis=0))
    inv_rms = jnp.concatenate([scales[:, 0:1], scales[:, 1:2]], axis=0)
    pull = jnp.concatenate([scales[:, 2:3], scales[:, 3:4]], axis=0)
    for h in range(heads):
        da = inv_rms * head(gained_ref, h) - head(att_ref, h).astype(F32) * pull
        da = da.astype(BF16)
        da_ref[:, h * DK : (h + 1) * DK] = da
        update = dot(flipped_ref[h], da, 1, 0)
        update_ref[h * pieces : (h + 1) * pieces] = update.reshape(pieces, -1, DK)


def grads_kernel(
    q_ref, k_ref, v_ref, ld_ref, state_ref, da_ref, dq_ref, kd_ref, fall_ref, dk_ref, dv_ref
):
    heads = ld_ref.shape[0]
    causal = triangle()
    low = causal.astype(F32).astype(BF16)
    columns = cum_columns(ld_ref[...], low)
    rows = cum_rows(ld_ref[...], low)
    rise = jnp.exp(columns)
    fall = jnp.exp(columns[BLOCK - 1 : BLOCK, :] - columns)
    for h in range(heads):
        here = slice(h * DK, (h + 1) * DK)
        q, k, da = head(q_ref, h), head(k_ref, h), head(da_ref, h)
        fall_wide = jnp.broadcast_to(fall[:, h : h + 1], (BLOCK, DK))
        fall_ref[:, here] = fall_wide
        kd_ref[:, here] = (k.astype(F32) * fall_wide).astype(BF16)
        mask = decay_mask(causal, columns, rows, h)
        scored = (dot(q, k, 1, 1) * mask).astype(BF16)
        d_scored = (dot(da, head(v_ref, h), 1, 1) * mask).astype(BF16)
        dq = dot(d_scored, k, 1, 0)
        dq += rise[:, h : h + 1] * dot(da, state_ref[h].astype(BF16), 1, 1)
        dq_ref[:, here] = dq.astype(BF16)
        dk_ref[:, here] = dot(d_scored, q, 0, 0)
        dv_ref[:, here] = dot(scored, da, 0, 0)


def final_kernel(
    dk_local_ref, dv_local_ref, v_ref, kd_ref, fall_ref, grad_ref, dk_hbm, dv_hbm, dk_ref, dv_ref, sems
):
    heads = grad_ref.shape[0]
    copies = []
    for h in range(heads):
        here = (slice(None), slice(h * DK, (h + 1) * DK))
        grad = grad_ref[h].astype(BF16)
        dk = head(dk_local_ref, h) + head(fall_ref, h) * dot(head(v_ref, h), grad, 1, 1)
        dk_ref[here] = dk.astype(BF16)
        dv = head(dv_local_ref, h) + dot(head(kd_ref, h), grad, 1, 0)
        dv_ref[here] = dv.astype(BF16)
        copies.append(pltpu.make_async_copy(dk_ref.at[here], dk_hbm.at[here], sems.at[2 * h]))
        copies.append(pltpu.make_async_copy(dv_ref.at[here], dv_hbm.at[here], sems.at[2 * h + 1]))
        copies[-2].start()
        copies[-1].start()
    for copy in copies:
        copy.wait()


def call(kernel, outs, flops, *args, **kinds):
    moved = sum(math.prod(a.shape) * 4 for a in (*args, *outs))
    return pl.pallas_call(
        kernel,
        out_shape=outs,
        compiler_params=pltpu.CompilerParams(vmem_limit_bytes=8 << 20),
        cost_estimate=pl.CostEstimate(flops=flops, bytes_accessed=moved, transcendentals=0),
        **kinds,
    )(*args)


IN_HBM = pl.BlockSpec(memory_space=pltpu.HBM)


def shape(dims, dtype=F32):
    return jax.ShapeDtypeStruct(dims, dtype)


def member_order(size, first):
    return [(first + place) % size for place in range(size)]


def exchange(array, axis, order):
    return lax.all_to_all(array, axis, 0, 0, axis_index_groups=[order], tiled=True)


def shards(query_rows, key_rows, value_rows, log_decay, norm_gain, d_normed):
    heads = log_decay.shape[0]
    ctx, tp = lax.axis_size("ctx"), lax.axis_size("tp")
    wide = heads * DK
    piece = heads * DK // ctx
    pieces = (ctx, piece, DK)
    rows = (BLOCK, wide)
    unit = 2 * heads * BLOCK * DK * DK
    gain = norm_gain.reshape(1, wide)
    order = member_order(ctx, ctx // 2 + 6)
    chips = member_order(tp // 2, tp // 2 - 2)
    tp_order = [chip * 2 + core for core in (1, 0) for chip in chips]
    places = [order.index(block) for block in range(ctx)]

    packed = call(
        update_kernel,
        (shape((ctx, piece + 1, 1, DK)),),
        unit,
        *(pltpu.with_memory_space_constraint(x, pltpu.HBM) for x in (key_rows, value_rows, log_decay)),
        in_specs=[IN_HBM] * 3,
        scratch_shapes=[
            pltpu.VMEM(rows, BF16),
            pltpu.VMEM(rows, BF16),
            pltpu.VMEM(log_decay.shape, F32),
            pltpu.SemaphoreType.DMA((3,)),
        ],
    )[0]
    packed = exchange(packed, "ctx", order)
    fades = packed[:, piece:, 0, :]
    before = call(
        functools.partial(scan_kernel, places),
        (shape(pieces),),
        unit // 32,
        fades,
        packed[:, :piece, 0, :],
    )[0]
    q_decayed, flipped, local, gained = call(
        local_kernel,
        (shape(rows, BF16), shape((heads, DK, BLOCK), BF16), shape(rows), shape(rows)),
        6 * unit,
        query_rows,
        key_rows,
        value_rows,
        log_decay,
        gain,
        d_normed,
    )
    states = exchange(before, "ctx", order).reshape(heads, DK, DK)
    attended, sums = call(
        attend_kernel,
        (shape(rows, BF16), shape((tp, 4, DK))),
        unit,
        local,
        q_decayed,
        states,
        gained,
    )
    sums = exchange(sums, "tp", tp_order)
    d_attended, updates = call(
        norm_kernel,
        (shape(rows, BF16), shape(pieces)),
        unit,
        attended,
        flipped,
        gained,
        sums,
    )
    after = call(
        functools.partial(scan_kernel, places[::-1]),
        (shape(pieces),),
        unit // 32,
        fades,
        exchange(updates, "ctx", order),
    )[0]
    d_query, k_decayed, fall, dk_local, dv_local = call(
        grads_kernel,
        (shape(rows, BF16), shape(rows, BF16), shape(rows), shape(rows), shape(rows)),
        12 * unit,
        query_rows,
        key_rows,
        value_rows,
        log_decay,
        states,
        d_attended,
    )
    grads = exchange(after, "ctx", order).reshape(heads, DK, DK)
    d_key, d_value = call(
        final_kernel,
        (shape(rows, BF16), shape(rows, BF16)),
        2 * unit,
        dk_local,
        dv_local,
        value_rows,
        k_decayed,
        fall,
        grads,
        out_specs=(IN_HBM, IN_HBM),
        scratch_shapes=[
            pltpu.VMEM(rows, BF16),
            pltpu.VMEM(rows, BF16),
            pltpu.SemaphoreType.DMA((2 * heads,)),
        ],
    )
    return d_query, d_key, d_value


def solution(mesh):
    placed = (
        P("ctx", "tp"),
        P("ctx", "tp"),
        P("ctx", "tp"),
        P("tp", "ctx"),
        P("tp"),
        P("ctx", "tp"),
    )
    return jax.shard_map(
        shards,
        mesh=mesh,
        in_specs=placed,
        out_specs=(P("ctx", "tp"), P("ctx", "tp"), P("ctx", "tp")),
        check_vma=False,
    )
```
